32 devices in a mesh: groups: 2 (over x), seq: 16 (over z, y, core).
Axes of the slice: x: 2, y: 2, z: 4, core: 2. Of those that a mesh axis runs over, the one named last changes fastest.
Arguments:
- cache_keys: bfloat16 [131072, 1024], P(('groups', 'seq')), parts along dimension 0, may hold values from -48 to 48
- cache_values: bfloat16 [131072, 1024], P(('groups', 'seq')), parts along dimension 0, may hold values from -6 to 6
- sketch_matrix: float32 [1024, 160], replicated, may hold values from -6 to 6
- queries: bfloat16 [6, 8192], P('groups'), parts along dimension 0, may hold values from -2000 to 2000
- fresh_keys: bfloat16 [6, 1024], P('groups'), parts along dimension 0, may hold values from -20 to 20
- fresh_values: bfloat16 [6, 1024], P('groups'), parts along dimension 0, may hold values from -6 to 6
- chosen: int32 [6, 8, 256], P('groups'), parts along dimension 0, may hold values from 0 to 8191, as said below
- shard_counts: int32 [6, 8, 16], P('groups'), parts along dimension 0, may hold values from 0 to 48, as said below
- outliers: int32 [64], P('groups'), parts along dimension 0, may hold values from 0 to 8191, as said below
Outputs:
- attended: bfloat16 [6, 8192], P('groups', 'seq'), parts along dimension 0
- key_factor: float32 [131072, 160], P(('groups', 'seq')), parts along dimension 0
The draws below stay inside these ranges and needn't reach their ends.
There are 2 independent parts, one for each index of `groups`. The reference program is written for one: setup_inputs(seed, part) draws one part's arguments, and reference() takes and returns one part's arrays. A program takes and returns all parts, laid end to end along the dimension named above; an argument that names none is the same for every part. Nothing has to cross between parts.
Inputs may be any that keep to these rules, and one draw needn't show every extreme that they name: Each list chosen[t, g] holds distinct span numbers in ascending order, none of them an outlier span; shard s holds spans s * 512 to (s+1) * 512 - 1. shard_counts[t, g, s] is the number of entries of chosen[t, g] on shard s; they sum to 256; the most is 48, reached in every list. `outliers`: distinct span numbers in ascending order; at most 4 on one shard, reached on some shard.
All inputs are finite; a program needn't handle non-finite values.
Results may differ from the reference program's by a relative error of at most 0.0228.
Values may be sent and summed in bfloat16 or wider, within the bound.
A program may use at most 128 MiB of HBM per device.

```python
import jax
import jax.numpy as jnp
from jax import lax

KVH = 8
HD = 128
QH = 64
RANK = 160
SPAN = 8
STEPS = 3
SEL = 256
OUTL = 32
OMOST = 4
LEN_DEV = 4096
D_KV = 1024
GROUP = 8
LENGTH = 65536
CH_DEV = 512
TOTAL_CH = 8192
MOST = 48
N_SEQ = 16


def capped_deal(deal_key, total_items, cap_items, weights_row):
    hot_key, loop_key = jax.random.split(deal_key)
    hottest = jax.random.randint(hot_key, (), 0, N_SEQ)
    tally = jnp.zeros((N_SEQ,), jnp.int32).at[hottest].set(cap_items)

    def place_one(item_turn, tally_now):
        open_weight = jnp.where(tally_now >= cap_items, 0, weights_row)
        running = jnp.cumsum(open_weight)
        ticket = jax.random.randint(jax.random.fold_in(loop_key, item_turn), (), 0, running[-1])
        target_shard = jnp.sum((running <= ticket).astype(jnp.int32))
        return tally_now.at[target_shard].add(1)
    return lax.fori_loop(0, total_items - cap_items, place_one, tally)


def shard_ranks(rank_key, pushed):
    span_ids = jnp.arange(TOTAL_CH, dtype=jnp.int32)
    shard_of = span_ids // CH_DEV
    shuffled = jax.random.permutation(rank_key, TOTAL_CH).astype(jnp.int32)
    order_pos = jnp.zeros((TOTAL_CH,), jnp.int32).at[shuffled].set(span_ids)
    sort_key = shard_of * (2 * TOTAL_CH) + pushed * TOTAL_CH + order_pos
    ordering = jnp.argsort(sort_key)
    placed = jnp.zeros((TOTAL_CH,), jnp.int32).at[ordering].set(span_ids)
    return placed - shard_of * CH_DEV


def selection_tables(key):
    base_key = jax.random.fold_in(key, 7177)
    out_key, sel_key = jax.random.split(base_key)
    out_deal, out_rank = jax.random.split(out_key)
    outlier_counts = capped_deal(out_deal, OUTL, OMOST, jnp.ones((N_SEQ,), jnp.int32))
    span_ids = jnp.arange(TOTAL_CH, dtype=jnp.int32)
    shard_of = span_ids // CH_DEV
    outlier_rank = shard_ranks(out_rank, jnp.zeros((TOTAL_CH,), jnp.int32))
    is_outlier = outlier_rank < outlier_counts[shard_of]
    outlier_list = jnp.sort(jnp.where(is_outlier, span_ids, TOTAL_CH + span_ids))[:OUTL]

    def one_list(list_key):
        weight_key, deal_key, order_key = jax.random.split(list_key, 3)
        raw_weight = jax.random.randint(weight_key, (N_SEQ,), 1, 9)
        tally = capped_deal(deal_key, SEL, MOST, raw_weight * raw_weight)
        ranks = shard_ranks(order_key, is_outlier.astype(jnp.int32))
        taken = (ranks < tally[shard_of]) & jnp.logical_not(is_outlier)
        return (jnp.sort(jnp.where(taken, span_ids, TOTAL_CH + span_ids))[:SEL], tally)
    lists, tallies = jax.vmap(one_list)(jax.random.split(sel_key, STEPS * KVH))
    return (lists.reshape(STEPS, KVH, SEL), tallies.reshape(STEPS, KVH, N_SEQ), outlier_list)


def query_tables(key):
    base_key = jax.random.fold_in(key, 3131)
    key_query, key_fresh = jax.random.split(base_key, 2)
    query_rows = jnp.clip(jax.random.normal(key_query, (STEPS, QH, HD), jnp.float32), -5.0, 5.0)
    fresh_rows = jnp.clip(jax.random.normal(key_fresh, (STEPS, KVH, HD), jnp.float32), -5.0, 5.0)
    group_sum = jnp.sum(query_rows.reshape(STEPS, KVH, QH // KVH, HD), axis=2) / jnp.sqrt(jnp.float32(QH // KVH))
    strength = 5.0 * jnp.sqrt(jnp.float32(QH // KVH) / jnp.float32(HD))
    fresh_rows = jnp.clip(strength * group_sum + 0.3 * fresh_rows, -20.0, 20.0)
    return (query_rows.reshape(STEPS, QH * HD), fresh_rows.reshape(STEPS, KVH * HD))


def draw_cache_keys(key, part):
    raw_keys = jnp.clip(jax.random.normal(jax.random.fold_in(key, 5151), (LENGTH, D_KV), jnp.float32), -6.0, 6.0)
    levels = jnp.exp(jax.random.uniform(jax.random.fold_in(key, 5252), (D_KV,), jnp.float32, minval=jnp.log(0.5), maxval=jnp.log(2.0)))
    shard_of = jnp.arange(LENGTH, dtype=jnp.int32) // LEN_DEV
    block_of = jnp.arange(D_KV, dtype=jnp.int32) // (D_KV // N_SEQ)
    offset = (block_of[None, :] - shard_of[:, None]) % N_SEQ
    paired = (offset == 0) | (offset == 1) | (offset == N_SEQ // 2) | (offset == N_SEQ // 2 + 1)
    return (raw_keys * jnp.where(paired, 4.0, 1.0) * levels[None, :]).astype(jnp.bfloat16)


def draw_chosen(key, part):
    return selection_tables(key)[0]


def draw_shard_counts(key, part):
    return selection_tables(key)[1]


def draw_outliers(key, part):
    return selection_tables(key)[2]


def draw_queries(key, part):
    return query_tables(key)[0].astype(jnp.bfloat16)


def draw_fresh_keys(key, part):
    return query_tables(key)[1].astype(jnp.bfloat16)


def steps_of(rng, dims, cuts, least, largest):
    factor_of, own = 1.0, jax.random.fold_in(rng, 6)
    for dim, parts in cuts:
        draws = jnp.exp(jax.random.uniform(jax.random.fold_in(own, dim), (parts,), jnp.float32, least / len(cuts), largest / len(cuts)))
        factor_of = factor_of * jnp.repeat(draws, dims[dim] // parts).reshape([-1 if axis == dim else 1 for axis in range(len(dims))])
    return factor_of


def noise(stream_key, dims, scale, bound, shards=(), kind=jnp.bfloat16):
    result = jax.random.normal(stream_key, dims, jnp.float32) * scale
    if len(shards) > 0:
        result = steps_of(stream_key, dims, shards, -0.22, 0.18) * result
    return jnp.clip(result, min=-bound, max=bound).astype(kind)


def setup_inputs(seed: int = 0, part: int = 0) -> dict:
    streams_of = jax.random.split(jax.random.key(seed), 10)
    own_keys = jax.random.split(jax.random.fold_in(streams_of[9], part), 10)
    cache_keys = draw_cache_keys(jax.random.fold_in(jax.random.fold_in(streams_of[9], part), 71), part)
    cache_values = noise(own_keys[1], (LENGTH, D_KV), 1.0, 6.0, ((0, 16),))
    sketch_matrix = noise(streams_of[2], (D_KV, RANK), 1.0, 6.0, (), jnp.float32)
    queries = draw_queries(jax.random.fold_in(jax.random.fold_in(streams_of[9], part), 71), part)
    fresh_keys = draw_fresh_keys(jax.random.fold_in(jax.random.fold_in(streams_of[9], part), 71), part)
    fresh_values = noise(own_keys[5], (STEPS, D_KV), 1.0, 6.0)
    chosen = draw_chosen(jax.random.fold_in(jax.random.fold_in(streams_of[9], part), 71), part)
    shard_counts = draw_shard_counts(jax.random.fold_in(jax.random.fold_in(streams_of[9], part), 71), part)
    outliers = draw_outliers(jax.random.fold_in(jax.random.fold_in(streams_of[9], part), 71), part)
    return {"cache_keys": cache_keys, "cache_values": cache_values, "sketch_matrix": sketch_matrix, "queries": queries, "fresh_keys": fresh_keys, "fresh_values": fresh_values, "chosen": chosen, "shard_counts": shard_counts, "outliers": outliers}


def rotate(vectors, positions):
    half_width = vectors.shape[-1] // 2
    exponents = jnp.arange(half_width, dtype=jnp.float32) * (2.0 / vectors.shape[-1])
    inverse_freq = jnp.exp(-jnp.log(jnp.float32(500000.0)) * exponents)
    angles = positions.astype(jnp.float32)[..., None] * inverse_freq
    cosine = jnp.cos(angles)
    sine = jnp.sin(angles)
    first_half = vectors[..., :half_width]
    second_half = vectors[..., half_width:]
    return jnp.concatenate([first_half * cosine - second_half * sine, second_half * cosine + first_half * sine], axis=-1)

def make_basis(sketch):
    small_gram = jnp.dot(sketch.T, sketch, precision=lax.Precision.HIGHEST)
    lower = jnp.linalg.cholesky(small_gram)
    solved = lax.linalg.triangular_solve(lower, sketch.T, left_side=True, lower=True)
    return solved.T.astype(jnp.bfloat16)

def reference(cache_keys, cache_values, sketch_matrix, queries, fresh_keys, fresh_values, chosen, shard_counts, outliers):
    contract = (((0,), (0,)), ((), ()))
    gram_total = lax.dot_general(cache_keys.astype(jnp.float32), cache_keys.astype(jnp.float32), contract, preferred_element_type=jnp.float32) / LENGTH
    sketch = jnp.dot(gram_total, sketch_matrix, precision=lax.Precision.HIGHEST)
    key_basis = make_basis(sketch)
    key_factor = jnp.dot(cache_keys.astype(jnp.float32), key_basis.astype(jnp.float32), preferred_element_type=jnp.float32)
    preceding = jnp.cumsum(shard_counts, axis=2) - shard_counts
    padded_list = jnp.concatenate([chosen, jnp.zeros((STEPS, KVH, MOST), jnp.int32)], axis=2)
    slot_ids = jnp.arange(MOST, dtype=jnp.int32)
    place = (preceding[..., None] + slot_ids).reshape(STEPS, KVH, N_SEQ * MOST)
    picked = jnp.take_along_axis(padded_list, place, axis=2).reshape(STEPS, KVH, N_SEQ, MOST)
    is_live = slot_ids < shard_counts[..., None]
    shard_base = (jnp.arange(N_SEQ, dtype=jnp.int32) * CH_DEV)[:, None]
    span_ids = jnp.clip(picked - shard_base, 0, CH_DEV - 1) + shard_base
    span_ids = span_ids.reshape(STEPS, KVH, N_SEQ * MOST)
    is_live = is_live.reshape(STEPS, KVH, N_SEQ * MOST)
    factor_spans = key_factor.reshape(TOTAL_CH, SPAN, RANK)[span_ids]
    basis_heads = key_basis.reshape(KVH, HD, RANK)
    rebuilt = jnp.einsum('tgmcr,gdr->tgmcd', factor_spans.astype(jnp.float32), basis_heads.astype(jnp.float32), precision=lax.Precision.HIGHEST)
    token_pos = span_ids[..., None] * SPAN + jnp.arange(SPAN, dtype=jnp.int32)
    sel_keys = rotate(rebuilt, token_pos).astype(jnp.bfloat16)
    value_blocks = cache_values.reshape(TOTAL_CH, SPAN, KVH, HD)
    head_ids = jnp.arange(KVH, dtype=jnp.int32)
    sel_values = value_blocks[span_ids, :, head_ids[None, :, None], :]
    key_blocks = cache_keys.reshape(TOTAL_CH, SPAN, KVH, HD)
    out_keys = key_blocks[outliers[None, :], :, head_ids[:, None], :]
    out_pos = outliers[:, None] * SPAN + jnp.arange(SPAN, dtype=jnp.int32)
    out_keys = rotate(out_keys.astype(jnp.float32), out_pos).astype(jnp.bfloat16)
    out_values = value_blocks[outliers[None, :], :, head_ids[:, None], :]
    all_keys = jnp.concatenate([sel_keys.reshape(STEPS, KVH, -1, HD), jnp.broadcast_to(out_keys.reshape(1, KVH, -1, HD), (STEPS, KVH, OUTL * SPAN, HD))], axis=2)
    all_values = jnp.concatenate([sel_values.reshape(STEPS, KVH, -1, HD), jnp.broadcast_to(out_values.reshape(1, KVH, -1, HD), (STEPS, KVH, OUTL * SPAN, HD))], axis=2)
    live_tokens = jnp.concatenate([jnp.repeat(is_live, SPAN, axis=2), jnp.ones((STEPS, KVH, OUTL * SPAN), bool)], axis=2)
    step_pos = LENGTH + jnp.arange(STEPS, dtype=jnp.int32)
    query_rows = rotate(queries.reshape(STEPS, QH, HD).astype(jnp.float32), step_pos[:, None]).reshape(STEPS, KVH, GROUP, HD)
    new_keys = rotate(fresh_keys.reshape(STEPS, KVH, HD).astype(jnp.float32), step_pos[:, None]).astype(jnp.bfloat16)
    new_values = fresh_values.reshape(STEPS, KVH, HD)
    score_scale = 1.0 / jnp.sqrt(jnp.float32(HD))
    cache_scores = jnp.einsum('tgqd,tgld->tgql', query_rows, all_keys.astype(jnp.float32), precision=lax.Precision.HIGHEST) * score_scale
    cache_scores = jnp.where(live_tokens[:, :, None, :], cache_scores, -1e+30)
    new_scores = jnp.einsum('tgqd,sgd->tgqs', query_rows, new_keys.astype(jnp.float32), precision=lax.Precision.HIGHEST) * score_scale
    causal = jnp.arange(STEPS)[None, :] <= jnp.arange(STEPS)[:, None]
    new_scores = jnp.where(causal[:, None, None, :], new_scores, -1e+30)
    row_max = jnp.maximum(lax.optimization_barrier(jnp.max(cache_scores, axis=-1)), lax.optimization_barrier(jnp.max(new_scores, axis=-1)))
    cache_weights = jnp.exp(cache_scores - row_max[..., None]) * live_tokens[:, :, None, :]
    new_weights = jnp.exp(new_scores - row_max[..., None]) * causal[:, None, None, :]
    totals = lax.optimization_barrier(jnp.sum(cache_weights, axis=-1)) + lax.optimization_barrier(jnp.sum(new_weights, axis=-1))
    summed = jnp.einsum('tgql,tgld->tgqd', cache_weights, all_values.astype(jnp.float32), precision=lax.Precision.HIGHEST)
    summed = summed + jnp.einsum('tgqs,sgd->tgqd', new_weights, new_values.astype(jnp.float32), precision=lax.Precision.HIGHEST)
    attended = (summed / totals[..., None]).reshape(STEPS, QH * HD).astype(jnp.bfloat16)
    return (attended, key_factor)
```

```python
import functools

import jax
import jax.numpy as jnp
from jax import lax
from jax.experimental import pallas as pl
from jax.experimental.pallas import tpu as pltpu
from jax.sharding import PartitionSpec as P

KVH = 8
HD = 128
QH = 64
SPAN = 8
OMOST = 4
HALF = HD // 2
LANES = 128
VMEM_LIMIT = 60 * 1024 * 1024
MESH = pl.DeviceIdType.MESH
NT = (((1,), (1,)), ((), ()))
NN = (((1,), (0,)), ((), ()))


def dot(a, b, dims=NN, precision=None):
    return lax.dot_general(a, b, dims, precision=precision, preferred_element_type=jnp.float32)


def pieces(x, count):
    parts = []
    for _ in range(count):
        part = x.astype(jnp.bfloat16)
        parts.append(part)
        x = x - part.astype(jnp.float32)
    return parts


def vmem(shape=None, index=None):
    if shape is None:
        return pl.BlockSpec(memory_space=pltpu.VMEM)
    return pl.BlockSpec(shape, index)


def sketch_kernel(length, s_ref, k_ref, out_ref, terms, acc):
    step = pl.program_id(0)
    rank = s_ref.shape[0]

    @pl.when(step == 0)
    def _():
        for i, part in enumerate(pieces(s_ref[...], 3)):
            terms[i * rank : (i + 1) * rank, :] = part

    keys = k_ref[...]
    wide = dot(terms[...], keys, NT)
    coords = wide[:rank] + wide[rank : 2 * rank] + wide[2 * rank :]
    high, low = pieces(coords, 2)
    share = dot(high, keys) + dot(low, keys)

    @pl.when(step == 0)
    def _():
        acc[...] = share

    @pl.when(step > 0)
    def _():
        acc[...] = acc[...] + share

    @pl.when(step == pl.num_programs(0) - 1)
    def _():
        total = acc[...] / length
        for c in range(out_ref.shape[1]):
            out_ref[:, c, :] = total[:, c * LANES : (c + 1) * LANES]


def sketch_part(s_t, cache_keys, length):
    rank, width = s_t.shape
    chunk = min(1024, cache_keys.shape[0])
    return pl.pallas_call(
        functools.partial(sketch_kernel, length),
        grid=(cache_keys.shape[0] // chunk,),
        out_shape=jax.ShapeDtypeStruct((rank, width // LANES, LANES), jnp.float32),
        in_specs=[vmem((rank, width), lambda i: (0, 0)), vmem((chunk, width), lambda i: (i, 0))],
        out_specs=vmem((rank, width // LANES, LANES), lambda i: (0, 0, 0)),
        scratch_shapes=[
            pltpu.VMEM((3 * rank, width), jnp.bfloat16),
            pltpu.VMEM((rank, width), jnp.float32),
        ],
        compiler_params=pltpu.CompilerParams(vmem_limit_bytes=VMEM_LIMIT),
        name="sketch_part",
    )(s_t, cache_keys)


def sum_kernel(
    chips, x_ref, out_ref, from_core, staged, inbox, full,
    core_s, core_r, chip_s, chip_r, back_s, back_r, fwd_s, fwd_r,
):
    me = lax.axis_index("seq")
    core = lax.rem(me, 2)
    chip = me // 2
    other = 1 - core
    partner = {"seq": chip * 2 + other}

    def chip_at(off):
        return lax.rem(chip + off, chips)

    def peer(off):
        return {"seq": chip_at(off) * 2 + core}

    barrier = pltpu.get_barrier_semaphore()
    pl.semaphore_signal(barrier, inc=1, device_id=partner, device_id_type=MESH)
    for off in range(1, chips):
        pl.semaphore_signal(barrier, inc=1, device_id=peer(off), device_id_type=MESH)
    pl.semaphore_wait(barrier, chips)

    def remote(src, dst, send, recv, target):
        return pltpu.make_async_remote_copy(
            src_ref=src, dst_ref=dst, send_sem=send, recv_sem=recv,
            device_id=target, device_id_type=MESH,
        )

    order = list(range(1, chips)) + [0]
    crossed = {}
    for off in order:
        crossed[off] = remote(
            x_ref.at[other, chip_at(off)], from_core.at[off], core_s.at[off], core_r.at[off], partner
        )
        crossed[off].start()
    sent = {}
    for off in order:
        crossed[off].wait_recv()
        staged[off] = x_ref[core, chip_at(off)] + from_core[off]
        if off:
            sent[off] = remote(
                staged.at[off], inbox.at[off], chip_s.at[off], chip_r.at[off], peer(off)
            )
            sent[off].start()
    total = staged[0]
    for off in range(1, chips):
        sent[off].wait_recv()
        total = total + inbox[off]
    full[core, chip] = total
    back = {}
    for off in range(1, chips):
        back[off] = remote(
            full.at[core, chip], full.at[core, chip], back_s.at[off], back_r.at[off], peer(off)
        )
        back[off].start()
    forward = {}
    for off in range(chips):
        source = chip_at(chips - off)
        if off:
            pltpu.make_async_remote_copy(
                src_ref=full.at[core, source], dst_ref=full.at[core, source],
                send_sem=back_s.at[off], recv_sem=back_r.at[off],
                device_id=peer(off), device_id_type=MESH,
            ).wait_recv()
        forward[off] = remote(
            full.at[core, source], full.at[core, source], fwd_s.at[off], fwd_r.at[off], partner
        )
        forward[off].start()
    for off in range(chips):
        source = chip_at(chips - off)
        pltpu.make_async_remote_copy(
            src_ref=full.at[other, source], dst_ref=full.at[other, source],
            send_sem=fwd_s.at[off], recv_sem=fwd_r.at[off],
            device_id=partner, device_id_type=MESH,
        ).wait_recv()
    out_ref[...] = full[...]
    for off in range(chips):
        crossed[off].wait_send()
        forward[off].wait_send()
        if off:
            sent[off].wait_send()
            back[off].wait_send()


def sum_over_seq(x, devices):
    chips = devices // 2
    shape = (2, chips, x.shape[0] // devices) + x.shape[1:]
    block = shape[1:]
    dma = pltpu.SemaphoreType.DMA((chips,))
    summed = pl.pallas_call(
        functools.partial(sum_kernel, chips),
        out_shape=jax.ShapeDtypeStruct(shape, jnp.float32),
        in_specs=[vmem()],
        out_specs=vmem(),
        scratch_shapes=[
            pltpu.VMEM(block, jnp.float32),
            pltpu.VMEM(block, jnp.float32),
            pltpu.VMEM(block, jnp.float32),
            pltpu.VMEM(shape, jnp.float32),
        ]
        + [dma] * 8,
        compiler_params=pltpu.CompilerParams(
            collective_id=0, has_side_effects=True, vmem_limit_bytes=VMEM_LIMIT
        ),
        name="sketch_sum",
    )(x.reshape(shape))
    return summed.reshape(x.shape)


def basis_kernel(sk_ref, basis_ref, split_ref, sk, a_ref, e_ref, inv_ref):
    rank = sk.shape[0]
    block = 32 if rank % 32 == 0 else 8
    high = lax.Precision.HIGHEST
    for c in range(sk_ref.shape[1]):
        sk[:, c * LANES : (c + 1) * LANES] = sk_ref[:, c, :]
    a_ref[...] = dot(sk[...], sk[...], NT, high)
    row = lax.broadcasted_iota(jnp.int32, (rank, rank), 0)
    column = lax.broadcasted_iota(jnp.int32, (rank, rank), 1)
    e_ref[...] = jnp.where(row == column, 1.0, 0.0)
    local = lax.broadcasted_iota(jnp.int32, (block, 1), 0)
    diagonal = lax.broadcasted_iota(jnp.int32, (block, rank), 1) - lax.broadcasted_iota(
        jnp.int32, (block, rank), 0
    )
    for top in range(0, rank, block):
        a = a_ref[top : top + block, :]
        e = e_ref[top : top + block, :]
        for j in range(block):
            pivot = a[j : j + 1, top + j : top + j + 1]
            factor = jnp.where(local > j, a[:, top + j : top + j + 1] / pivot, 0.0)
            a = a - factor * a[j : j + 1, :]
            e = e - factor * e[j : j + 1, :]
        pivots = jnp.sum(jnp.where(diagonal == top, a, 0.0), axis=1, keepdims=True)
        scale = 1.0 / jnp.sqrt(pivots)
        a = a * scale
        e = e * scale
        inv_ref[top : top + block, :] = e
        low = top + block
        if low < rank:
            a_t = a.T[low:, :]
            a_ref[low:, :] -= dot(a_t, a, NN, high)
            e_ref[low:, :] -= dot(a_t, e, NN, high)
    basis = dot(inv_ref[...], sk[...], NN, high)
    basis_ref[...] = basis.astype(jnp.bfloat16)
    for p in range(basis.shape[1] // (2 * HD)):
        pair = basis[:, p * 2 * HD : (p + 1) * 2 * HD]
        split_ref[:, p * 2 * HD : (p + 1) * 2 * HD] = jnp.concatenate(
            [
                pair[:, :HALF],
                pair[:, HD : HD + HALF],
                pair[:, HALF:HD],
                pair[:, HD + HALF :],
            ],
            axis=1,
        ).astype(jnp.bfloat16)


def make_basis(sketch_t):
    rank = sketch_t.shape[0]
    width = sketch_t.shape[1] * LANES
    shape = jax.ShapeDtypeStruct((rank, width), jnp.bfloat16)
    return pl.pallas_call(
        basis_kernel,
        out_shape=(shape, shape),
        in_specs=[vmem()],
        out_specs=(vmem(), vmem()),
        scratch_shapes=[
            pltpu.VMEM((rank, width), jnp.float32),
            pltpu.VMEM((rank, rank), jnp.float32),
            pltpu.VMEM((rank, rank), jnp.float32),
            pltpu.VMEM((rank, rank), jnp.float32),
        ],
        compiler_params=pltpu.CompilerParams(vmem_limit_bytes=VMEM_LIMIT),
        name="key_basis",
    )(sketch_t)


def attend_kernel(
    k_ref, v_ref, basis_ref, split_ref, q_ref, live_ref, ca_ref, sa_ref, cb_ref, sb_ref,
    xk_ref, xv_ref, xlive_ref, factor_ref, out_ref, max_ref, sum_ref, terms, spread,
):
    step = pl.program_id(0)
    pairs, rows, width = q_ref.shape
    chunk = k_ref.shape[0]
    spans = spread.shape[0]

    @pl.when(step == 0)
    def _():
        for p in range(pairs):
            for i, part in enumerate(pieces(q_ref[p], 3)):
                terms[p, i * rows : (i + 1) * rows, :] = part
        token = lax.broadcasted_iota(jnp.int32, (spans, chunk), 1)
        span = lax.broadcasted_iota(jnp.int32, (spans, chunk), 0)
        spread[...] = jnp.where(token // SPAN == span, 1.0, 0.0).astype(jnp.bfloat16)
        out_ref[...] = jnp.zeros_like(out_ref)
        sum_ref[...] = jnp.zeros_like(sum_ref)
        max_ref[...] = jnp.full(max_ref.shape, -1e30, jnp.float32)

    def absorb(p, keys, values, live):
        here = slice(p * rows, (p + 1) * rows)
        wide = dot(terms[p], keys, NT)
        scores = wide[:rows] + wide[rows : 2 * rows] + wide[2 * rows :]
        scores = jnp.where(live > 0.5, scores, -1e30)
        before = max_ref[here, :]
        after = jnp.maximum(before, jnp.max(scores, axis=1, keepdims=True))
        weights = jnp.where(live > 0.5, jnp.exp(scores - after[:, :1]), 0.0)
        scale = jnp.exp(before - after)
        max_ref[here, :] = after
        sum_ref[here, :] = sum_ref[here, :] * scale + jnp.sum(weights, axis=1, keepdims=True)
        both = dot(jnp.concatenate(pieces(weights, 2), axis=0), values)
        both = both[:rows] + both[rows:]
        own = jnp.concatenate([both[: rows // 2, :HD], both[rows // 2 :, HD:]], axis=0)
        out_ref[here, :] = out_ref[here, :] * scale + own

    factor = dot(k_ref[...], basis_ref[...], NT)
    factor_ref[...] = factor
    high, low = pieces(factor, 2)
    cb, sb = cb_ref[...], sb_ref[...]
    cosine, sine = [], []
    for i in range(ca_ref.shape[0]):
        ca, sa = ca_ref[i : i + 1, :], sa_ref[i : i + 1, :]
        cosine.append(ca * cb - sa * sb)
        sine.append(sa * cb + ca * sb)
    cosine = jnp.concatenate(cosine, axis=0)
    sine = jnp.concatenate(sine, axis=0)
    for p in range(pairs):
        columns = slice(p * width, (p + 1) * width)
        rebuilt = dot(high, split_ref[:, columns]) + dot(low, split_ref[:, columns])
        first, second = rebuilt[:, :HD], rebuilt[:, HD:]
        keys = jnp.concatenate(
            [first * cosine - second * sine, second * cosine + first * sine], axis=1
        ).astype(jnp.bfloat16)
        live = dot(live_ref[p * rows : (p + 1) * rows, :], spread[...])
        absorb(p, keys, v_ref[:, columns], live)

    @pl.when(step == pl.num_programs(0) - 1)
    def _():
        for p in range(pairs):
            columns = slice(p * width, (p + 1) * width)
            live = xlive_ref[p * rows : (p + 1) * rows, :]
            absorb(p, xk_ref[:, columns], xv_ref[:, columns], live)


def attend(cache_keys, cache_values, basis, split, q, live, tables, xk, xv, xlive):
    seq_len, width = cache_keys.shape
    rank = basis.shape[0]
    pairs, rows, pair_width = q.shape
    chunk = min(LANES * SPAN, seq_len)
    spans = chunk // SPAN
    fine = tables[2].shape[0]
    total = pairs * rows
    whole = lambda *shape: vmem(shape, lambda i: (0,) * len(shape))
    stat = jax.ShapeDtypeStruct((total, LANES), jnp.float32)
    return pl.pallas_call(
        attend_kernel,
        grid=(seq_len // chunk,),
        out_shape=(jax.ShapeDtypeStruct((seq_len, rank), jnp.float32), stat, stat, stat),
        in_specs=[
            vmem((chunk, width), lambda i: (i, 0)),
            vmem((chunk, width), lambda i: (i, 0)),
            whole(rank, width),
            whole(rank, width),
            whole(pairs, rows, pair_width),
            vmem((total, spans), lambda i: (0, i)),
            vmem((chunk // fine, LANES), lambda i: (i, 0)),
            vmem((chunk // fine, LANES), lambda i: (i, 0)),
            whole(fine, LANES),
            whole(fine, LANES),
            whole(*xk.shape),
            whole(*xv.shape),
            whole(*xlive.shape),
        ],
        out_specs=(vmem((chunk, rank), lambda i: (i, 0)),) + (whole(total, LANES),) * 3,
        scratch_shapes=[
            pltpu.VMEM((pairs, 3 * rows, pair_width), jnp.bfloat16),
            pltpu.VMEM((spans, chunk), jnp.bfloat16),
        ],
        compiler_params=pltpu.CompilerParams(vmem_limit_bytes=VMEM_LIMIT),
        name="attend",
    )(cache_keys, cache_values, basis, split, q, live, *tables, xk, xv, xlive)


def merge_kernel(devices, x_ref, out_ref, inbox, send_sem, recv_sem):
    me = lax.axis_index("seq")
    rows = out_ref.shape[0]

    def peer(off):
        return lax.rem(me + off, devices)

    barrier = pltpu.get_barrier_semaphore()
    for off in range(1, devices):
        pl.semaphore_signal(
            barrier, inc=1, device_id={"seq": peer(off)}, device_id_type=MESH
        )
    pl.semaphore_wait(barrier, devices - 1)
    copies = []
    for off in range(1, devices):
        copy = pltpu.make_async_remote_copy(
            src_ref=x_ref.at[peer(off)], dst_ref=inbox.at[off],
            send_sem=send_sem.at[off], recv_sem=recv_sem.at[off],
            device_id={"seq": peer(off)}, device_id_type=MESH,
        )
        copy.start()
        copies.append(copy)
    own = x_ref[me]
    for copy in copies:
        copy.wait_recv()
    blocks = [own] + [inbox[off] for off in range(1, devices)]
    maxima = [block[rows:, :1] for block in blocks]
    joint = functools.reduce(jnp.maximum, maxima)
    total = jnp.zeros((rows, 1), jnp.float32)
    summed = jnp.zeros((rows, HD), jnp.float32)
    for block, top in zip(blocks, maxima):
        scale = jnp.exp(top - joint)
        total = total + block[rows:, HALF : HALF + 1] * scale
        summed = summed + block[:rows, :] * scale
    out_ref[...] = (summed / total).astype(out_ref.dtype)
    for copy in copies:
        copy.wait_send()


def merge(x):
    devices, rows, lanes = x.shape
    return pl.pallas_call(
        functools.partial(merge_kernel, devices),
        out_shape=jax.ShapeDtypeStruct((rows // 2, lanes), jnp.bfloat16),
        in_specs=[vmem()],
        out_specs=vmem(),
        scratch_shapes=[
            pltpu.VMEM(x.shape, jnp.float32),
            pltpu.SemaphoreType.DMA((devices,)),
            pltpu.SemaphoreType.DMA((devices,)),
        ],
        compiler_params=pltpu.CompilerParams(collective_id=1, has_side_effects=True),
        name="merge",
    )(x)


def waves(positions):
    exponents = jnp.arange(HALF, dtype=jnp.float32) * (2.0 / HD)
    inverse_freq = jnp.exp(-jnp.log(jnp.float32(500000.0)) * exponents)
    angles = positions.astype(jnp.float32)[..., None] * inverse_freq
    return jnp.cos(angles), jnp.sin(angles)


def rotate_halves(vectors, positions):
    cosine, sine = waves(positions)
    first, second = vectors[..., :HALF], vectors[..., HALF:]
    return jnp.stack([first * cosine - second * sine, second * cosine + first * sine], axis=-2)


def on_device(
    cache_keys,
    cache_values,
    sketch_matrix,
    queries,
    fresh_keys,
    fresh_values,
    chosen,
    shard_counts,
    outliers,
):
    seq_len, width = cache_keys.shape
    devices = lax.axis_size("seq")
    myself = lax.axis_index("seq")
    length = seq_len * devices
    steps = queries.shape[0]
    group = QH // KVH
    per_device = QH // devices
    pairs = KVH // 2
    spans_dev = seq_len // SPAN
    base = myself * spans_dev

    share = sketch_part(sketch_matrix.T, cache_keys, length)
    basis, split = make_basis(sum_over_seq(share, devices))

    own_spans = base + jnp.arange(spans_dev, dtype=jnp.int32)
    live = jnp.any(chosen[..., None] == own_spans, axis=2)
    live = jnp.broadcast_to(
        live.transpose(1, 0, 2)[:, :, None, :], (KVH, steps, group, spans_dev)
    ).reshape(KVH * steps * group, spans_dev).astype(jnp.bfloat16)

    outlier_here = outliers // spans_dev == myself
    order = jnp.cumsum(outlier_here.astype(jnp.int32)) - 1
    match = outlier_here & (order == jnp.arange(OMOST, dtype=jnp.int32)[:, None])
    local = jnp.sum(jnp.where(match, outliers - base, 0), axis=1)
    outlier_live = jnp.any(match, axis=1)
    exact = [lax.dynamic_slice_in_dim(cache_keys, local[i] * SPAN, SPAN, 0) for i in range(OMOST)]
    exact_v = [
        lax.dynamic_slice_in_dim(cache_values, local[i] * SPAN, SPAN, 0) for i in range(OMOST)
    ]
    step_pos = length + jnp.arange(steps, dtype=jnp.int32)
    token = jnp.arange(SPAN, dtype=jnp.int32)
    extra_pos = jnp.concatenate([((local + base)[:, None] * SPAN + token).reshape(-1), step_pos])
    count = OMOST * SPAN + steps
    pad = ((0, LANES - count), (0, 0))
    xk = jnp.concatenate(exact + [fresh_keys], axis=0).reshape(count, KVH, HD)
    xk = rotate_halves(xk.astype(jnp.float32), extra_pos[:, None])
    xk = xk.reshape(count, pairs, 2, 2, HALF).transpose(0, 1, 3, 2, 4).reshape(count, width)
    xk = jnp.pad(xk.astype(jnp.bfloat16), pad)
    xv = jnp.pad(jnp.concatenate(exact_v + [fresh_values], axis=0), pad)
    causal = jnp.arange(steps)[None, :] <= jnp.arange(steps)[:, None]
    extra_live = jnp.concatenate(
        [
            jnp.broadcast_to(jnp.repeat(outlier_live, SPAN), (steps, OMOST * SPAN)),
            causal & (myself == 0),
        ],
        axis=1,
    )
    xlive = jnp.pad(extra_live.astype(jnp.float32), ((0, 0), (0, LANES - count)))
    xlive = jnp.broadcast_to(
        xlive[None, :, None, :], (KVH, steps, group, LANES)
    ).reshape(KVH * steps * group, LANES)

    score_scale = 1.0 / jnp.sqrt(jnp.float32(HD))
    q = rotate_halves(queries.reshape(steps, QH, HD).astype(jnp.float32), step_pos[:, None])
    q = (q * score_scale).reshape(steps, pairs, 2, group, 2, HALF).transpose(1, 2, 0, 3, 4, 5)
    own_lane = jnp.eye(2, dtype=jnp.float32)[None, :, None, None, None, :, None]
    q = (q[:, :, :, :, :, None, :] * own_lane).reshape(pairs, 2 * steps * group, 2 * HD)

    fine = 64
    coarse = jnp.arange(seq_len // fine, dtype=jnp.int32) * fine + myself * seq_len
    tables = waves(coarse) + waves(jnp.arange(fine, dtype=jnp.int32))
    tables = [jnp.concatenate([table, table], axis=1) for table in tables]

    key_factor, out, top, total = attend(
        cache_keys, cache_values, basis, split, q, live, tables, xk, xv, xlive
    )

    def deal(x):
        x = x.reshape(KVH, steps, group // per_device, per_device, LANES)
        return x.transpose(0, 2, 1, 3, 4).reshape(devices, steps * per_device, LANES)

    stats = jnp.where(jnp.arange(LANES) < HALF, top, total)
    attended = merge(jnp.concatenate([deal(out), deal(stats)], axis=1))
    return (attended.reshape(steps, per_device * HD), key_factor)


def solution(mesh):
    in_specs = (
        P(("groups", "seq"), None),
        P(("groups", "seq"), None),
        P(),
        P("groups", None),
        P("groups", None),
        P("groups", None),
        P("groups", None, None),
        P("groups", None, None),
        P("groups"),
    )
    out_specs = (P("groups", "seq"), P(("groups", "seq"), None))
    return jax.shard_map(
        on_device, mesh=mesh, in_specs=in_specs, out_specs=out_specs, check_vma=False
    )
```

```python
import functools

import jax
import jax.numpy as jnp
from jax import lax
from jax.experimental import pallas as pl
from jax.experimental.pallas import tpu as pltpu
from jax.sharding import PartitionSpec as P

KVH = 8
HD = 128
QH = 64
SPAN = 8
OMOST = 4
HALF = HD // 2
FINE = 64
LANES = 128
VMEM_LIMIT = 60 * 1024 * 1024
MESH = pl.DeviceIdType.MESH
NT = (((1,), (1,)), ((), ()))
NN = (((1,), (0,)), ((), ()))


def dot(a, b, dims=NN, precision=None):
    return lax.dot_general(a, b, dims, precision=precision, preferred_element_type=jnp.float32)


def pieces(x, count):
    parts = []
    for _ in range(count):
        part = x.astype(jnp.bfloat16)
        parts.append(part)
        x = x - part.astype(jnp.float32)
    return parts


def vmem(shape=None, index=None):
    if shape is None:
        return pl.BlockSpec(memory_space=pltpu.VMEM)
    return pl.BlockSpec(shape, index)


def sketch_kernel(length, s_ref, k_ref, out_ref, terms, acc):
    step = pl.program_id(0)
    rank = s_ref.shape[0]

    @pl.when(step == 0)
    def _():
        for i, part in enumerate(pieces(s_ref[...], 3)):
            terms[i * rank : (i + 1) * rank, :] = part

    keys = k_ref[...]
    wide = dot(terms[...], keys, NT)
    coords = wide[:rank] + wide[rank : 2 * rank] + wide[2 * rank :]
    high, low = pieces(coords, 2)
    share = dot(high, keys) + dot(low, keys)

    @pl.when(step == 0)
    def _():
        acc[...] = share

    @pl.when(step > 0)
    def _():
        acc[...] = acc[...] + share

    @pl.when(step == pl.num_programs(0) - 1)
    def _():
        total = acc[...] / length
        for c in range(out_ref.shape[1]):
            out_ref[:, c, :] = total[:, c * LANES : (c + 1) * LANES]


def sketch_part(s_t, cache_keys, length):
    rank, width = s_t.shape
    chunk = min(1024, cache_keys.shape[0])
    return pl.pallas_call(
        functools.partial(sketch_kernel, length),
        grid=(cache_keys.shape[0] // chunk,),
        out_shape=jax.ShapeDtypeStruct((rank, width // LANES, LANES), jnp.float32),
        in_specs=[vmem((rank, width), lambda i: (0, 0)), vmem((chunk, width), lambda i: (i, 0))],
        out_specs=vmem((rank, width // LANES, LANES), lambda i: (0, 0, 0)),
        scratch_shapes=[
            pltpu.VMEM((3 * rank, width), jnp.bfloat16),
            pltpu.VMEM((rank, width), jnp.float32),
        ],
        compiler_params=pltpu.CompilerParams(vmem_limit_bytes=VMEM_LIMIT),
        name="sketch_part",
    )(s_t, cache_keys)


def sum_kernel(
    chips, x_ref, out_ref, from_core, staged, inbox, full,
    core_s, core_r, chip_s, chip_r, back_s, back_r, fwd_s, fwd_r,
):
    me = lax.axis_index("seq")
    core = lax.rem(me, 2)
    chip = me // 2
    other = 1 - core
    partner = {"seq": chip * 2 + other}

    def chip_at(off):
        return lax.rem(chip + off, chips)

    def peer(off):
        return {"seq": chip_at(off) * 2 + core}

    barrier = pltpu.get_barrier_semaphore()
    pl.semaphore_signal(barrier, inc=1, device_id=partner, device_id_type=MESH)
    for off in range(1, chips):
        pl.semaphore_signal(barrier, inc=1, device_id=peer(off), device_id_type=MESH)
    pl.semaphore_wait(barrier, chips)

    def remote(src, dst, send, recv, target):
        return pltpu.make_async_remote_copy(
            src_ref=src, dst_ref=dst, send_sem=send, recv_sem=recv,
            device_id=target, device_id_type=MESH,
        )

    order = list(range(1, chips)) + [0]
    crossed = {}
    for off in order:
        crossed[off] = remote(
            x_ref.at[other, chip_at(off)], from_core.at[off], core_s.at[off], core_r.at[off], partner
        )
        crossed[off].start()
    sent = {}
    for off in order:
        crossed[off].wait_recv()
        staged[off] = x_ref[core, chip_at(off)] + from_core[off]
        if off:
            sent[off] = remote(
                staged.at[off], inbox.at[off], chip_s.at[off], chip_r.at[off], peer(off)
            )
            sent[off].start()
    total = staged[0]
    for off in range(1, chips):
        sent[off].wait_recv()
        total = total + inbox[off]
    full[core, chip] = total
    back = {}
    for off in range(1, chips):
        back[off] = remote(
            full.at[core, chip], full.at[core, chip], back_s.at[off], back_r.at[off], peer(off)
        )
        back[off].start()
    forward = {}
    for off in range(chips):
        source = chip_at(chips - off)
        if off:
            pltpu.make_async_remote_copy(
                src_ref=full.at[core, source], dst_ref=full.at[core, source],
                send_sem=back_s.at[off], recv_sem=back_r.at[off],
                device_id=peer(off), device_id_type=MESH,
            ).wait_recv()
        forward[off] = remote(
            full.at[core, source], full.at[core, source], fwd_s.at[off], fwd_r.at[off], partner
        )
        forward[off].start()
    for off in range(chips):
        source = chip_at(chips - off)
        pltpu.make_async_remote_copy(
            src_ref=full.at[other, source], dst_ref=full.at[other, source],
            send_sem=fwd_s.at[off], recv_sem=fwd_r.at[off],
            device_id=partner, device_id_type=MESH,
        ).wait_recv()
    out_ref[...] = full[...]
    for off in range(chips):
        crossed[off].wait_send()
        forward[off].wait_send()
        if off:
            sent[off].wait_send()
            back[off].wait_send()


def sum_over_seq(x, devices):
    chips = devices // 2
    shape = (2, chips, x.shape[0] // devices) + x.shape[1:]
    block = shape[1:]
    dma = pltpu.SemaphoreType.DMA((chips,))
    summed = pl.pallas_call(
        functools.partial(sum_kernel, chips),
        out_shape=jax.ShapeDtypeStruct(shape, jnp.float32),
        in_specs=[vmem()],
        out_specs=vmem(),
        scratch_shapes=[
            pltpu.VMEM(block, jnp.float32),
            pltpu.VMEM(block, jnp.float32),
            pltpu.VMEM(block, jnp.float32),
            pltpu.VMEM(shape, jnp.float32),
        ]
        + [dma] * 8,
        compiler_params=pltpu.CompilerParams(
            collective_id=0, has_side_effects=True, vmem_limit_bytes=VMEM_LIMIT
        ),
        name="sketch_sum",
    )(x.reshape(shape))
    return summed.reshape(x.shape)


def basis_kernel(sk_ref, basis_ref, split_ref, sk, a_ref, e_ref, inv_ref):
    rank = sk.shape[0]
    block = 32 if rank % 32 == 0 else 8
    high = lax.Precision.HIGHEST
    for c in range(sk_ref.shape[1]):
        sk[:, c * LANES : (c + 1) * LANES] = sk_ref[:, c, :]
    a_ref[...] = dot(sk[...], sk[...], NT, high)
    row = lax.broadcasted_iota(jnp.int32, (rank, rank), 0)
    column = lax.broadcasted_iota(jnp.int32, (rank, rank), 1)
    e_ref[...] = jnp.where(row == column, 1.0, 0.0)
    local = lax.broadcasted_iota(jnp.int32, (block, 1), 0)
    diagonal = lax.broadcasted_iota(jnp.int32, (block, rank), 1) - lax.broadcasted_iota(
        jnp.int32, (block, rank), 0
    )
    for top in range(0, rank, block):
        a = a_ref[top : top + block, :]
        e = e_ref[top : top + block, :]
        for j in range(block):
            pivot = a[j : j + 1, top + j : top + j + 1]
            factor = jnp.where(local > j, a[:, top + j : top + j + 1] / pivot, 0.0)
            a = a - factor * a[j : j + 1, :]
            e = e - factor * e[j : j + 1, :]
        pivots = jnp.sum(jnp.where(diagonal == top, a, 0.0), axis=1, keepdims=True)
        scale = 1.0 / jnp.sqrt(pivots)
        a = a * scale
        e = e * scale
        inv_ref[top : top + block, :] = e
        low = top + block
        if low < rank:
            a_t = a.T[low:, :]
            a_ref[low:, :] -= dot(a_t, a, NN, high)
            e_ref[low:, :] -= dot(a_t, e, NN, high)
    basis = dot(inv_ref[...], sk[...], NN, high)
    basis_ref[...] = basis.astype(jnp.bfloat16)
    for p in range(basis.shape[1] // (2 * HD)):
        pair = basis[:, p * 2 * HD : (p + 1) * 2 * HD]
        split_ref[:, p * 2 * HD : (p + 1) * 2 * HD] = jnp.concatenate(
            [
                pair[:, :HALF],
                pair[:, HD : HD + HALF],
                pair[:, HALF:HD],
                pair[:, HD + HALF :],
            ],
            axis=1,
        ).astype(jnp.bfloat16)


def make_basis(sketch_t):
    rank = sketch_t.shape[0]
    width = sketch_t.shape[1] * LANES
    shape = jax.ShapeDtypeStruct((rank, width), jnp.bfloat16)
    return pl.pallas_call(
        basis_kernel,
        out_shape=(shape, shape),
        in_specs=[vmem()],
        out_specs=(vmem(), vmem()),
        scratch_shapes=[
            pltpu.VMEM((rank, width), jnp.float32),
            pltpu.VMEM((rank, rank), jnp.float32),
            pltpu.VMEM((rank, rank), jnp.float32),
            pltpu.VMEM((rank, rank), jnp.float32),
        ],
        compiler_params=pltpu.CompilerParams(vmem_limit_bytes=VMEM_LIMIT),
        name="key_basis",
    )(sketch_t)


def split_pair(x):
    first = jnp.concatenate([x[:, :HALF], x[:, HD : HD + HALF]], axis=1)
    second = jnp.concatenate([x[:, HALF:HD], x[:, HD + HALF :]], axis=1)
    return first, second


def turn(first, second, cosine, sine):
    return jnp.concatenate(
        [first * cosine - second * sine, second * cosine + first * sine], axis=1
    )


def attend_kernel(
    outl_ref, k_ref, v_ref, k_all, v_all, basis_ref, split_ref, q_ref, live_ref, cos_ref,
    sin_ref, fresh_k, fresh_v, factor_ref, deal_ref,
    terms, spread, widen, out_ref, max_ref, sum_ref, cosines, sines, xk_land, xv_land, xk, xv,
    local_ref, sems,
):
    step = pl.program_id(0)
    steps = fresh_k.shape[0]
    width = 2 * HD
    pairs = k_ref.shape[1] // width
    group = QH // KVH
    list_rows = steps * group
    rows = 2 * list_rows
    chunk = k_ref.shape[0]
    spans = spread.shape[0]
    spans_dev = k_all.shape[0] // SPAN
    coarse = spans_dev * SPAN // FINE
    myself = lax.axis_index("seq")
    base = myself * spans_dev
    per_device = deal_ref.shape[1] // (2 * steps)

    @pl.when(step == 0)
    def _():
        for i in range(OMOST + 1):
            local_ref[i] = 0
        found = jnp.int32(0)
        for i in range(outl_ref.shape[0]):
            span = outl_ref[i] - base
            local_ref[found] = span
            here = (span >= 0) & (span < spans_dev)
            found = found + here.astype(jnp.int32)
        copies = []
        for j in range(OMOST):
            at = jnp.where(j < found, local_ref[j], 0)
            local_ref[j] = at
            for n, (whole, land) in enumerate(((k_all, xk_land), (v_all, xv_land))):
                copy = pltpu.make_async_copy(
                    whole.at[pl.ds(pl.multiple_of(at * SPAN, SPAN), SPAN), :],
                    land.at[j],
                    sems.at[n, j],
                )
                copy.start()
                copies.append(copy)
        local_ref[OMOST] = found

        cosines[...] = jnp.concatenate([cos_ref[...]] * 2, axis=1)
        sines[...] = jnp.concatenate([sin_ref[...]] * 2, axis=1)
        first_step = coarse + FINE
        zeros = jnp.zeros((list_rows, HALF), jnp.float32)
        for p in range(pairs):
            for side in range(2):
                head = (2 * p + side) * group
                turned = []
                for t in range(steps):
                    x = q_ref[t * QH + head : t * QH + head + group, :]
                    c = cos_ref[first_step + t : first_step + t + 1, :]
                    d = sin_ref[first_step + t : first_step + t + 1, :]
                    turned.append(turn(x[:, :HALF], x[:, HALF:], c, d))
                x = jnp.concatenate(turned, axis=0)
                x = [x[:, :HALF], zeros, x[:, HALF:], zeros]
                if side:
                    x = [x[1], x[0], x[3], x[2]]
                for i, part in enumerate(pieces(jnp.concatenate(x, axis=1), 3)):
                    at = i * rows + side * list_rows
                    terms[p, at : at + list_rows, :] = part.astype(jnp.float32)
        token = lax.broadcasted_iota(jnp.int32, (spans, chunk), 1)
        span = lax.broadcasted_iota(jnp.int32, (spans, chunk), 0)
        spread[...] = jnp.where(token // SPAN == span, 1.0, 0.0).astype(jnp.bfloat16)
        row = lax.broadcasted_iota(jnp.int32, widen.shape, 0)
        which = lax.broadcasted_iota(jnp.int32, widen.shape, 1)
        source = ((row % list_rows) // group) * KVH + row // list_rows
        widen[...] = jnp.where(which == source, 1.0, 0.0).astype(jnp.bfloat16)
        out_ref[...] = jnp.zeros_like(out_ref)
        sum_ref[...] = jnp.zeros_like(sum_ref)
        max_ref[...] = jnp.full(max_ref.shape, -1e30, jnp.float32)
        for copy in copies:
            copy.wait()

    def absorb(p, keys, values, live):
        here = slice(p * rows, (p + 1) * rows)
        wide = dot(terms[p].astype(jnp.bfloat16), keys, NT)
        scores = wide[:rows] + wide[rows : 2 * rows] + wide[2 * rows :]
        scores = jnp.where(live, scores, -1e30)
        before = max_ref[here, :]
        after = jnp.maximum(before, jnp.max(scores, axis=1, keepdims=True))
        weights = jnp.where(live, jnp.exp(scores - after[:, :1]), 0.0)
        scale = jnp.exp(before - after)
        max_ref[here, :] = after
        sum_ref[here, :] = sum_ref[here, :] * scale + jnp.sum(weights, axis=1, keepdims=True)
        both = dot(jnp.concatenate(pieces(weights, 2), axis=0), values)
        both = both[:rows] + both[rows:]
        own = jnp.concatenate([both[: rows // 2, :HD], both[rows // 2 :, HD:]], axis=0)
        out_ref[here, :] = out_ref[here, :] * scale + own

    factor = dot(k_ref[...], basis_ref[...], NT)
    factor_ref[...] = factor.T
    high, low = pieces(factor, 2)
    cb = cosines[coarse : coarse + FINE, :]
    sb = sines[coarse : coarse + FINE, :]
    cosine, sine = [], []
    for i in range(chunk // FINE):
        ca = cosines[pl.ds(step * (chunk // FINE) + i, 1), :]
        sa = sines[pl.ds(step * (chunk // FINE) + i, 1), :]
        cosine.append(ca * cb - sa * sb)
        sine.append(sa * cb + ca * sb)
    cosine = jnp.concatenate(cosine, axis=0)
    sine = jnp.concatenate(sine, axis=0)
    live_all = dot(widen[...], live_ref[...]).astype(jnp.bfloat16)
    for p in range(pairs):
        columns = slice(p * width, (p + 1) * width)
        rebuilt = dot(high, split_ref[:, columns]) + dot(low, split_ref[:, columns])
        keys = turn(rebuilt[:, :HD], rebuilt[:, HD:], cosine, sine).astype(jnp.bfloat16)
        live = dot(live_all[p * rows : (p + 1) * rows, :], spread[...])
        absorb(p, keys, v_ref[:, columns], live > 0.5)

    @pl.when(step == pl.num_programs(0) - 1)
    def _():
        exact = OMOST * SPAN
        xk[...] = jnp.zeros_like(xk)
        xv[...] = jnp.zeros_like(xv)
        for j in range(OMOST):
            xk[j * SPAN : (j + 1) * SPAN, :] = xk_land[j].astype(jnp.float32)
            xv[j * SPAN : (j + 1) * SPAN, :] = xv_land[j].astype(jnp.float32)
        xk[exact : exact + steps, :] = fresh_k[...].astype(jnp.float32)
        xv[exact : exact + steps, :] = fresh_v[...].astype(jnp.float32)
        xc, xs = [], []
        for j in range(OMOST):
            at = local_ref[j] * SPAN
            ca = cosines[pl.ds(at // FINE, 1), :]
            sa = sines[pl.ds(at // FINE, 1), :]
            near = pl.multiple_of(coarse + at % FINE, SPAN)
            cb = cosines[pl.ds(near, SPAN), :]
            sb = sines[pl.ds(near, SPAN), :]
            xc.append(ca * cb - sa * sb)
            xs.append(sa * cb + ca * sb)
        rest = jnp.zeros((LANES - exact - SPAN, LANES), jnp.float32)
        xc = jnp.concatenate(xc + [cosines[coarse + FINE :, :], rest], axis=0)
        xs = jnp.concatenate(xs + [sines[coarse + FINE :, :], rest], axis=0)
        row = lax.broadcasted_iota(jnp.int32, (rows, LANES), 0)
        lane = lax.broadcasted_iota(jnp.int32, (rows, LANES), 1)
        reach = jnp.where(myself == 0, exact, -LANES)
        own_step = (row % list_rows) // group
        live = (lane < local_ref[OMOST] * SPAN) | (
            (lane >= exact) & (lane <= reach + own_step)
        )
        for p in range(pairs):
            columns = slice(p * width, (p + 1) * width)
            first, second = split_pair(xk[:, columns])
            keys = turn(first, second, xc, xs).astype(jnp.bfloat16)
            absorb(p, keys, xv[:, columns].astype(jnp.bfloat16), live)
        half = steps * per_device
        lane = lax.broadcasted_iota(jnp.int32, out_ref.shape, 1)
        max_ref[...] = jnp.where(lane < HALF, max_ref[...], sum_ref[...])
        for device in range(deal_ref.shape[0]):
            for t in range(steps):
                head = device * per_device
                at = (head // group) * list_rows + t * group + head % group
                to = t * per_device
                deal_ref[device, to : to + per_device, :] = out_ref[at : at + per_device, :]
                deal_ref[device, half + to : half + to + per_device, :] = max_ref[
                    at : at + per_device, :
                ]


def attend(cache_keys, cache_values, basis, split, q, live, cosine, sine, fresh_k, fresh_v, outliers, devices):
    seq_len, width = cache_keys.shape
    rank = basis.shape[0]
    steps = fresh_k.shape[0]
    group = QH // KVH
    rows = 2 * steps * group
    pairs = KVH // 2
    chunk = min(LANES * SPAN, seq_len)
    spans = chunk // SPAN
    total = pairs * rows
    whole = lambda *shape: vmem(shape, lambda i: (0,) * len(shape))
    deal = (devices, 2 * steps * (QH // devices), LANES)
    anywhere = pl.BlockSpec(memory_space=pl.ANY)
    return pl.pallas_call(
        attend_kernel,
        grid=(seq_len // chunk,),
        out_shape=(
            jax.ShapeDtypeStruct((rank, seq_len), jnp.float32),
            jax.ShapeDtypeStruct(deal, jnp.float32),
        ),
        in_specs=[
            pl.BlockSpec(memory_space=pltpu.SMEM),
            vmem((chunk, width), lambda i: (i, 0)),
            vmem((chunk, width), lambda i: (i, 0)),
            anywhere,
            anywhere,
            whole(rank, width),
            whole(rank, width),
            whole(*q.shape),
            vmem((live.shape[0], spans), lambda i: (0, i)),
            whole(*cosine.shape),
            whole(*sine.shape),
            whole(*fresh_k.shape),
            whole(*fresh_v.shape),
        ],
        out_specs=(vmem((rank, chunk), lambda i: (0, i)), whole(*deal)),
        scratch_shapes=[
            pltpu.VMEM((pairs, 3 * rows, 2 * HD), jnp.float32),
            pltpu.VMEM((spans, chunk), jnp.bfloat16),
            pltpu.VMEM((total, live.shape[0]), jnp.bfloat16),
            pltpu.VMEM((total, LANES), jnp.float32),
            pltpu.VMEM((total, LANES), jnp.float32),
            pltpu.VMEM((total, LANES), jnp.float32),
            pltpu.VMEM((cosine.shape[0], LANES), jnp.float32),
            pltpu.VMEM((cosine.shape[0], LANES), jnp.float32),
            pltpu.VMEM((OMOST, SPAN, width), jnp.bfloat16),
            pltpu.VMEM((OMOST, SPAN, width), jnp.bfloat16),
            pltpu.VMEM((LANES, width), jnp.float32),
            pltpu.VMEM((LANES, width), jnp.float32),
            pltpu.SMEM((outliers.shape[0] + OMOST + 1,), jnp.int32),
            pltpu.SemaphoreType.DMA((2, OMOST)),
        ],
        compiler_params=pltpu.CompilerParams(vmem_limit_bytes=VMEM_LIMIT),
        name="attend",
    )(
        outliers, cache_keys, cache_values, cache_keys, cache_values, basis, split, q, live,
        cosine, sine, fresh_k, fresh_v,
    )


def merge_kernel(devices, x_ref, out_ref, inbox, send_sem, recv_sem):
    me = lax.axis_index("seq")
    rows = out_ref.shape[0]

    def peer(off):
        return lax.rem(me + off, devices)

    barrier = pltpu.get_barrier_semaphore()
    for off in range(1, devices):
        pl.semaphore_signal(
            barrier, inc=1, device_id={"seq": peer(off)}, device_id_type=MESH
        )
    pl.semaphore_wait(barrier, devices - 1)
    copies = []
    for off in range(1, devices):
        copy = pltpu.make_async_remote_copy(
            src_ref=x_ref.at[peer(off)], dst_ref=inbox.at[off],
            send_sem=send_sem.at[off], recv_sem=recv_sem.at[off],
            device_id={"seq": peer(off)}, device_id_type=MESH,
        )
        copy.start()
        copies.append(copy)
    own = x_ref[me]
    for copy in copies:
        copy.wait_recv()
    blocks = [own] + [inbox[off] for off in range(1, devices)]
    maxima = [block[rows:, :1] for block in blocks]
    joint = functools.reduce(jnp.maximum, maxima)
    total = jnp.zeros((rows, 1), jnp.float32)
    summed = jnp.zeros((rows, HD), jnp.float32)
    for block, top in zip(blocks, maxima):
        scale = jnp.exp(top - joint)
        total = total + block[rows:, HALF : HALF + 1] * scale
        summed = summed + block[:rows, :] * scale
    out_ref[...] = (summed / total).astype(out_ref.dtype)
    for copy in copies:
        copy.wait_send()


def merge(x):
    devices, rows, lanes = x.shape
    return pl.pallas_call(
        functools.partial(merge_kernel, devices),
        out_shape=jax.ShapeDtypeStruct((rows // 2, lanes), jnp.bfloat16),
        in_specs=[vmem()],
        out_specs=vmem(),
        scratch_shapes=[
            pltpu.VMEM(x.shape, jnp.float32),
            pltpu.SemaphoreType.DMA((devices,)),
            pltpu.SemaphoreType.DMA((devices,)),
        ],
        compiler_params=pltpu.CompilerParams(collective_id=1, has_side_effects=True),
        name="merge",
    )(x)


def waves(positions):
    exponents = jnp.arange(HALF, dtype=jnp.float32) * (2.0 / HD)
    inverse_freq = jnp.exp(-jnp.log(jnp.float32(500000.0)) * exponents)
    angles = positions.astype(jnp.float32)[..., None] * inverse_freq
    return jnp.cos(angles), jnp.sin(angles)


def on_device(
    cache_keys,
    cache_values,
    sketch_matrix,
    queries,
    fresh_keys,
    fresh_values,
    chosen,
    shard_counts,
    outliers,
):
    seq_len, width = cache_keys.shape
    devices = lax.axis_size("seq")
    myself = lax.axis_index("seq")
    length = seq_len * devices
    steps = queries.shape[0]
    per_device = QH // devices
    spans_dev = seq_len // SPAN
    base = myself * spans_dev

    share = sketch_part(sketch_matrix.T, cache_keys, length)
    basis, split = make_basis(sum_over_seq(share, devices))

    own_spans = base + jnp.arange(spans_dev, dtype=jnp.int32)
    live = jnp.any(chosen[..., None] == own_spans, axis=2)
    live = live.reshape(steps * KVH, spans_dev).astype(jnp.bfloat16)
    q = queries.astype(jnp.float32).reshape(steps * QH, HD) * (
        1.0 / jnp.sqrt(jnp.float32(HD))
    )
    place = jnp.arange(seq_len // FINE + FINE + SPAN, dtype=jnp.int32)
    coarse = seq_len // FINE
    positions = jnp.where(
        place < coarse,
        place * FINE + myself * seq_len,
        jnp.where(place < coarse + FINE, place - coarse, place - coarse - FINE + length),
    )
    cosine, sine = waves(positions)
    factor_t, parts = attend(
        cache_keys, cache_values, basis, split, q, live, cosine, sine, fresh_keys, fresh_values,
        outliers, devices,
    )
    attended = merge(parts)
    return (attended.reshape(steps, per_device * HD), factor_t.T)


def solution(mesh):
    in_specs = (
        P(("groups", "seq"), None),
        P(("groups", "seq"), None),
        P(),
        P("groups", None),
        P("groups", None),
        P("groups", None),
        P("groups", None, None),
        P("groups", None, None),
        P("groups"),
    )
    out_specs = (P("groups", "seq"), P(("groups", "seq"), None))
    return jax.shard_map(
        on_device, mesh=mesh, in_specs=in_specs, out_specs=out_specs, check_vma=False
    )
```
